512 devices in a mesh: dp: 32 (over y_hi, z), tm: 16 (over y_lo, x, core).
Axes of the slice: x: 4, y: 4 (y_hi: 2, y_lo: 2; y = y_hi * 2 + y_lo), z: 16, core: 2. Of those that a mesh axis runs over, the one named last changes fastest.
Arguments:
- frames: bfloat16 [32, 4096, 1536], P('dp', 'tm'), may hold values from -6 to 6
- lengths: int32 [32], P('dp'), may hold values from 1024 to 4096
- ln_gain: float32 [1536], replicated, may hold values from 0.1 to 1.9
- w_query: bfloat16 [1536, 768], P('dp'), may hold values from -0.15625 to 0.15625
- w_key: bfloat16 [1536, 768], P('dp'), may hold values from -0.15625 to 0.15625
- w_value: bfloat16 [1536, 768], P('dp'), may hold values from -0.15625 to 0.15625
- w_output: bfloat16 [768, 1536], P('dp'), may hold values from -0.21875 to 0.21875
- w_position: bfloat16 [1536, 768], P(None, 'tm'), may hold values from -0.15625 to 0.15625
- bias_content: float32 [8, 96], replicated, may hold values from -60 to 60, as said below
- bias_position: float32 [8, 96], replicated, may hold values from -3 to 3
Outputs:
- attended: bfloat16 [32, 4096, 1536], P('dp', 'tm')
The draws below stay inside these ranges and needn't reach their ends.
Inputs may be any that keep to these rules, and one draw needn't show every extreme that they name: `lengths`: number of valid frames of each utterance; later frames are padding. `bias_content`: content biases; in some draws they reach magnitudes near 60.
All inputs are finite; a program needn't handle non-finite values.
Results may differ from the reference program's by a relative error of at most 0.012.
The reference program's roundings to bfloat16 on the way count: a program that leaves them out, or rounds other values in their place, can miss the bound.
Values may be sent and summed in bfloat16 or wider, within the bound.
A program may use at most 64 MiB of HBM per device.

```python
import math
import jax
import jax.numpy as jnp
from jax import lax

D = 1536
HEADS = 8
HS = 96
UTTS = 32
NT = 4096
HD = 768
N_TM = 16


def draw_bias_content(key, part):
    return jnp.clip(0.5 * jax.random.normal(key, (HEADS, HS), jnp.float32), -3.0, 3.0)


def place_ends(values, stream_key, low, top_value):
    longest = values.shape.index(max(values.shape))
    spots = []
    for shift in (0, 1):
        where = [jax.random.randint(jax.random.fold_in(stream_key, axis), (), 0, length) for axis, length in enumerate(values.shape)]
        where[longest] = (where[longest] + shift) % values.shape[longest]
        spots.append(tuple(where))
    return values.at[spots[0]].set(low).at[spots[1]].set(top_value)


def block_levels(stream_key, dims, shards, least, largest):
    def one(dim, parts):
        draws = jax.random.uniform(jax.random.fold_in(jax.random.fold_in(stream_key, 6), dim), (parts,), jnp.float32, least / len(shards), largest / len(shards))
        return jnp.repeat(jnp.exp(draws), dims[dim] // parts).reshape((-1,) + (1,) * (len(dims) - dim - 1))

    gain = one(*shards[0])
    for cut in shards[1:]:
        gain = gain * one(*cut)
    return gain


def noise(key, extent, deviation, most, shards=(), kind=jnp.bfloat16):
    factor_of = block_levels(key, extent, shards, -0.22, 0.18) if shards else 1.0
    entries = jax.random.normal(key, extent, jnp.float32) * deviation * factor_of
    return jnp.minimum(jnp.maximum(entries, -most), most).astype(kind)


def setup_inputs(seed: int = 0) -> dict:
    seeds = jax.random.split(jax.random.key(seed), 11)
    frames = noise(seeds[0], (UTTS, NT, D), 1.0, 6.0, ((0, 32), (1, 16)))
    lengths = place_ends(jax.random.randint(seeds[1], (UTTS,), NT // 4, NT + 1), jax.random.fold_in(seeds[1], 1), NT // 4, NT).astype(jnp.int32)
    ln_gain = jnp.clip(1.0 + 0.18 * jax.random.normal(seeds[2], (D,), jnp.float32), 0.1, 1.9)
    w_query = noise(seeds[3], (D, HD), D ** -0.5, 0.15625, ((0, 32),))
    w_key = noise(seeds[4], (D, HD), D ** -0.5, 0.15625, ((0, 32),))
    w_value = noise(seeds[5], (D, HD), D ** -0.5, 0.15625, ((0, 32),))
    w_output = noise(seeds[6], (HD, D), HD ** -0.5, 0.21875, ((0, 32),))
    w_position = noise(seeds[7], (D, HD), D ** -0.5, 0.15625, ((1, 16),))
    bias_content = draw_bias_content(jax.random.fold_in(seeds[10], 71), 0)
    bias_position = noise(seeds[9], (HEADS, HS), 0.5, 3.0, (), jnp.float32)
    return {"frames": frames, "lengths": lengths, "ln_gain": ln_gain, "w_query": w_query, "w_key": w_key, "w_value": w_value, "w_output": w_output, "w_position": w_position, "bias_content": bias_content, "bias_position": bias_position}


epsilon = 1e-05
masked_score = -1e+30

def layer_norm(frame_rows, ln_gain):
    widened = frame_rows.astype(jnp.float32)
    row_mean = lax.optimization_barrier(jnp.mean(widened, axis=-1, keepdims=True))
    centered = widened - row_mean
    row_var = lax.optimization_barrier(jnp.mean(centered * centered, axis=-1, keepdims=True))
    return (centered * lax.rsqrt(row_var + epsilon) * ln_gain).astype(jnp.bfloat16)

def sinusoid(row_count, model_width):
    offsets = jnp.arange(row_count, dtype=jnp.float32) - (row_count // 2 - 1)
    half_width = model_width // 2
    frequency = jnp.exp(jnp.arange(half_width, dtype=jnp.float32) * (-2.0 * math.log(10000.0) / model_width))
    angles = offsets[:, None] * frequency[None, :]
    return jnp.concatenate([jnp.sin(angles), jnp.cos(angles)], axis=1).astype(jnp.bfloat16)

def rel_shift(position_full):
    block_len = position_full.shape[0]
    span_len = position_full.shape[1]
    skewed = position_full.reshape(-1)[:block_len * (span_len - 1)].reshape(block_len, span_len - 1)
    return skewed[:, block_len - 1:4 * block_len - 1]

def attend(query_proj, key_rows, value_rows, rel_heads, bias_content, bias_position, valid_len, first_pos):
    block_len = query_proj.shape[0]
    head_count, head_size = bias_content.shape
    query_pos = first_pos + jnp.arange(block_len, dtype=jnp.int32)
    key_pos = first_pos - block_len + jnp.arange(3 * block_len, dtype=jnp.int32)
    key_valid = (key_pos >= 0) & (key_pos < valid_len)
    query_valid = (query_pos < valid_len).astype(jnp.float32)
    split_query = query_proj.reshape(block_len, head_count, head_size).astype(jnp.float32)
    with_content = (split_query + bias_content[None]).astype(jnp.bfloat16).transpose(1, 0, 2)
    with_position = (split_query + bias_position[None]).astype(jnp.bfloat16).transpose(1, 0, 2)
    key_heads = key_rows.reshape(3 * block_len, head_count, head_size).transpose(1, 0, 2)
    value_heads = value_rows.reshape(3 * block_len, head_count, head_size).transpose(1, 0, 2)
    scale = 1.0 / math.sqrt(head_size)

    def one_head(operands):
        content_query, position_query, key_head, value_head, rel_head = operands
        content = jnp.dot(content_query, key_head.T, preferred_element_type=jnp.float32)
        shifted = rel_shift(jnp.dot(position_query, rel_head.T, preferred_element_type=jnp.float32))
        scores = jnp.where(key_valid[None, :], (content + shifted) * scale, masked_score)
        row_max = lax.optimization_barrier(jnp.max(scores, axis=1, keepdims=True))
        raised = jnp.exp(scores - row_max)
        totals = lax.optimization_barrier(jnp.sum(raised, axis=1, keepdims=True))
        weights = (raised / totals).astype(jnp.bfloat16)
        return jnp.dot(weights, value_head, preferred_element_type=jnp.float32)
    context = lax.map(one_head, (with_content, with_position, key_heads, value_heads, rel_heads))
    context = context.transpose(1, 0, 2) * query_valid[:, None, None]
    return context.astype(jnp.bfloat16).reshape(block_len, head_count * head_size)

def reference(frames, lengths, ln_gain, w_query, w_key, w_value, w_output, w_position, bias_content, bias_position):
    total_len = frames.shape[1]
    model_width = frames.shape[2]
    block_len = total_len // N_TM
    head_count, head_size = bias_content.shape
    relative = jnp.dot(sinusoid(4 * block_len, model_width), w_position, preferred_element_type=jnp.float32).astype(jnp.bfloat16)
    rel_heads = relative.reshape(4 * block_len, head_count, head_size).transpose(1, 0, 2)

    def one_utterance(operands):
        frame_rows, valid_len = operands
        normed = layer_norm(frame_rows, ln_gain)
        query_proj = jnp.dot(normed, w_query, preferred_element_type=jnp.float32).astype(jnp.bfloat16)
        key_proj = jnp.dot(normed, w_key, preferred_element_type=jnp.float32).astype(jnp.bfloat16)
        value_proj = jnp.dot(normed, w_value, preferred_element_type=jnp.float32).astype(jnp.bfloat16)
        key_padded = jnp.pad(key_proj, ((block_len, block_len), (0, 0)))
        value_padded = jnp.pad(value_proj, ((block_len, block_len), (0, 0)))

        def one_block(block_idx):
            first_pos = block_idx * block_len
            return attend(lax.dynamic_slice_in_dim(query_proj, first_pos, block_len, 0), lax.dynamic_slice_in_dim(key_padded, first_pos, 3 * block_len, 0), lax.dynamic_slice_in_dim(value_padded, first_pos, 3 * block_len, 0), rel_heads, bias_content, bias_position, valid_len, first_pos)
        context = lax.map(one_block, jnp.arange(N_TM, dtype=jnp.int32)).reshape(total_len, head_count * head_size)
        mixed_out = jnp.dot(context, w_output, preferred_element_type=jnp.float32)
        return (frame_rows.astype(jnp.float32) + mixed_out).astype(jnp.bfloat16)
    return lax.map(one_utterance, (frames, lengths))
```

```python
import math

import jax
import jax.numpy as jnp
from jax import lax
from jax.experimental import pallas as pl
from jax.experimental.pallas import tpu as pltpu
from jax.sharding import PartitionSpec as P

MESH = pl.DeviceIdType.MESH
epsilon = 1e-05
masked_score = -1e30
BF16 = jnp.bfloat16
F32 = jnp.float32

D = 1536
HS = 96
BLOCK = 256
HALF = 384
NX = 4
NY = 4
STEP_ROWS = 128
GROUP = 32


def mm(a, b):
    return jnp.dot(a, b, preferred_element_type=F32)


def mm_t(a, b):
    return lax.dot_general(a, b, (((1,), (1,)), ((), ())), preferred_element_type=F32)


def kernel(
    nz,
    frames_ref,
    len_ref,
    gain_ref,
    wq_ref,
    wk_ref,
    wv_ref,
    wo_ref,
    wpos_ref,
    bias_ref,
    table_ref,
    out_ref,
    normed,
    pack,
    packo,
    big,
    bigo,
    enc,
    rel_own,
    rel,
    keys,
    values,
    with_c,
    with_p,
    ctx_out,
    ctx,
    loc_sem,
    s0_send,
    s0_recv,
    zs,
    zr,
    xs,
    xr,
    ys,
    yr,
    ra_send,
    ra_recv,
    rx_send,
    rx_recv,
    h_send,
    h_recv,
    p_send,
    p_recv,
):
    dp = lax.axis_index("dp")
    tm = lax.axis_index("tm")
    y_hi = dp // nz
    z = dp % nz
    y_lo = tm // 8
    x = (tm % 8) // 2
    c = tm % 2
    y = y_hi * 2 + y_lo
    half = nz // 2

    def dev(xx, yy, zz, cc):
        return ((yy // 2) * nz + zz, (yy % 2) * 8 + xx * 2 + cc)

    x_r, x_l, x_o = (x + 1) % NX, (x + 3) % NX, (x + 2) % NX
    y_r, y_l, y_o = (y + 1) % NY, (y + 3) % NY, (y + 2) % NY
    z_r, z_l = (z + 1) % nz, (z + nz - 1) % nz
    y_mate = y_hi * 2 + (1 - y_lo)
    y_mirror = 3 - y
    place = y_lo * NX + x
    nxt, prv = (place + 1) % 8, (place + 7) % 8
    dev_next = dev(nxt % NX, y_hi * 2 + nxt // NX, z, c)
    dev_prev = dev(prv % NX, y_hi * 2 + prv // NX, z, c)
    partner = dev(x, y, z, 1 - c)

    locals_ = []
    base = pl.multiple_of(c * HALF, 128)
    for k, ref in enumerate((wq_ref, wk_ref, wv_ref)):
        for j in range(3):
            t = 3 * k + j
            locals_.append(
                pltpu.make_async_copy(
                    ref.at[:, pl.ds(base + 128 * j, 128)], pack.at[t], loc_sem.at[t]
                )
            )
    baseo = pl.multiple_of(c * 768, 128)
    for j in range(6):
        locals_.append(
            pltpu.make_async_copy(
                wo_ref.at[:, pl.ds(baseo + 128 * j, 128)], packo.at[j], loc_sem.at[9 + j]
            )
        )
    for cp in locals_:
        cp.start()

    barrier = pltpu.get_barrier_semaphore()
    peers = [
        dev(x_r, y, z, c),
        dev(x_l, y, z, c),
        dev(x, y_r, z, c),
        dev(x, y_l, z, c),
        dev(x, y, z_r, c),
        dev(x, y, z_l, c),
        partner,
        dev(x, y_mate, z, 1 - c),
        dev_next,
        dev_prev,
    ]
    for p in peers:
        pl.semaphore_signal(barrier, inc=1, device_id=p, device_id_type=MESH)

    for cp in locals_:
        cp.wait()
    pl.semaphore_wait(barrier, len(peers))

    def rows(zz):
        return pl.ds(pl.multiple_of(zz * 48, 16), 48)

    def orows(zz):
        return pl.ds(pl.multiple_of(zz * 24, 8), 24)

    own_tiles = (x, NX + y, 8)
    mir_tiles = (x, NX + y_mirror, 8)
    own_o = (y, 4, 5)
    mir_o = (y_mirror, 4, 5)
    mirror = dev(x, y_mirror, z, c)
    stage0 = []
    own_copies = []
    for i in range(3):
        stage0.append(
            pltpu.make_async_remote_copy(
                pack.at[mir_tiles[i]],
                big.at[mir_tiles[i], y_hi, rows(z), :],
                s0_send.at[i],
                s0_recv.at[i],
                device_id=mirror,
                device_id_type=MESH,
            )
        )
        stage0.append(
            pltpu.make_async_remote_copy(
                packo.at[mir_o[i]],
                bigo.at[c, mir_o[i], y_hi, orows(z), :],
                s0_send.at[3 + i],
                s0_recv.at[3 + i],
                device_id=mirror,
                device_id_type=MESH,
            )
        )
        own_copies.append(
            pltpu.make_async_copy(
                pack.at[own_tiles[i]], big.at[own_tiles[i], y_hi, rows(z), :], loc_sem.at[i]
            )
        )
        own_copies.append(
            pltpu.make_async_copy(
                packo.at[own_o[i]], bigo.at[c, own_o[i], y_hi, orows(z), :], loc_sem.at[3 + i]
            )
        )
    for cp in stage0:
        cp.start()
    for cp in own_copies:
        cp.start()

    widened = frames_ref[...].astype(F32)
    row_mean = jnp.mean(widened, axis=-1, keepdims=True)
    centered = widened - row_mean
    row_var = jnp.mean(centered * centered, axis=-1, keepdims=True)
    own_rows = pl.ds(pl.multiple_of(c * BLOCK, BLOCK), BLOCK)
    normed[own_rows, :] = (centered * lax.rsqrt(row_var + epsilon) * gain_ref[...]).astype(BF16)
    send_normed = pltpu.make_async_remote_copy(
        normed.at[own_rows, :],
        normed.at[own_rows, :],
        p_send.at[0],
        p_recv.at[0],
        device_id=partner,
        device_id_type=MESH,
    )
    send_normed.start()

    for cp in own_copies:
        cp.wait()
    for i in range(3):
        pltpu.make_async_remote_copy(
            pack.at[own_tiles[i]],
            big.at[own_tiles[i], 1 - y_hi, rows(z), :],
            s0_send.at[i],
            s0_recv.at[i],
            device_id=mirror,
            device_id_type=MESH,
        ).wait_recv()
        pltpu.make_async_remote_copy(
            packo.at[own_o[i]],
            bigo.at[c, own_o[i], 1 - y_hi, orows(z), :],
            s0_send.at[3 + i],
            s0_recv.at[3 + i],
            device_id=mirror,
            device_id_type=MESH,
        ).wait_recv()

    def zview(lane, zz):
        if lane < 3:
            return big.at[own_tiles[lane], :, rows(zz), :]
        if lane == 3:
            return bigo.at[c, y, :, orows(zz), :]
        return bigo.at[c, 4:6, :, orows(zz), :]

    def zcopy(lane, way, zz):
        view = zview(lane, zz)
        return pltpu.make_async_remote_copy(
            view,
            view,
            zs.at[way, lane, zz],
            zr.at[lane, zz],
            device_id=dev(x, y, z_r if way == 0 else z_l, c),
            device_id_type=MESH,
        )

    def xcopy(kind, tile, zz, to):
        view = big.at[tile, :, rows(zz), :]
        return pltpu.make_async_remote_copy(
            view,
            view,
            xs.at[kind, zz],
            xr.at[kind, zz],
            device_id=dev(to, y, z, c),
            device_id_type=MESH,
        )

    def ycopy(lane, kind, tile, zz, to):
        view = big.at[NX + tile, :, rows(zz), :] if lane == 0 else bigo.at[c, tile, :, orows(zz), :]
        return pltpu.make_async_remote_copy(
            view,
            view,
            ys.at[lane, kind, zz],
            yr.at[lane, kind, zz],
            device_id=dev(x, to, z, c),
            device_id_type=MESH,
        )

    def spread(zz):
        xcopy(0, x, zz, x_r).start()
        xcopy(1, x, zz, x_l).start()
        for lane in range(2):
            ycopy(lane, 0, y, zz, y_r).start()
            ycopy(lane, 1, y, zz, y_l).start()

    def pass_on(way, zz):
        if way == 0:
            xcopy(0, x_l, zz, x_r).wait_recv()
            xcopy(2, x_l, zz, x_r).start()
            for lane in range(2):
                ycopy(lane, 0, y_l, zz, y_r).wait_recv()
                ycopy(lane, 2, y_l, zz, y_r).start()
        else:
            xcopy(1, x_r, zz, x_l).wait_recv()
            xcopy(2, x_r, zz, x_l).start()
            for lane in range(2):
                ycopy(lane, 1, y_r, zz, y_l).wait_recv()
                ycopy(lane, 2, y_r, zz, y_l).start()

    def rel_piece(s):
        for g in range(STEP_ROWS // GROUP):
            i = s * (STEP_ROWS // GROUP) + g
            sa = table_ref[0, pl.ds(i, 1), :]
            ca = table_ref[1, pl.ds(i, 1), :]
            sb = table_ref[2]
            cb = table_ref[3]
            enc[g * GROUP : (g + 1) * GROUP, 0:768] = (sa * cb + ca * sb).astype(BF16)
            enc[g * GROUP : (g + 1) * GROUP, 768:1536] = (ca * cb - sa * sb).astype(BF16)
        piece = mm(enc[...], wpos_ref[...])
        rel_own[:, pl.ds(pl.multiple_of(s * STEP_ROWS, STEP_ROWS), STEP_ROWS)] = piece.T.astype(BF16)

    pieces = 1024 // STEP_ROWS

    def step(s, carry):
        up = (z + nz - s) % nz
        down = (z + s) % nz
        for lane in range(5):

            @pl.when(s > 0)
            def _():
                zcopy(lane, 0, up).wait_recv()

            @pl.when(s < half)
            def _():
                zcopy(lane, 0, up).start()

            @pl.when((s > 0) & (s < half))
            def _():
                zcopy(lane, 1, down).wait_recv()

            @pl.when(s < half - 1)
            def _():
                zcopy(lane, 1, down).start()

        spread(up)

        @pl.when((s > 0) & (s < half))
        def _():
            spread(down)

        @pl.when(s > 0)
        def _():
            pass_on(0, (z + nz - s + 1) % nz)

        @pl.when(s > 1)
        def _():
            pass_on(1, (z + s - 1) % nz)

        @pl.when(s < pieces)
        def _():
            rel_piece(s)

        return carry

    lax.fori_loop(0, half + 1, step, 0)
    pass_on(0, (z + half) % nz)

    slot = pl.ds(pl.multiple_of(x * HS + c * 48, 16), 48)
    rel_cross = pltpu.make_async_remote_copy(
        rel_own,
        rel.at[slot, :],
        ra_send.at[0],
        ra_recv.at[c],
        device_id=dev(x, y_mate, z, y_lo),
        device_id_type=MESH,
    )
    rel_cross.start()
    rel_here = pltpu.make_async_copy(rel_own, rel.at[slot, :], loc_sem.at[0])
    rel_across = pltpu.make_async_remote_copy(
        rel_own,
        rel.at[slot, :],
        ra_send.at[1],
        ra_recv.at[c],
        device_id=partner,
        device_id_type=MESH,
    )

    @pl.when(c == y_lo)
    def _():
        rel_here.start()

    @pl.when(c != y_lo)
    def _():
        rel_across.start()

    def collect(zz, carry):
        offset = (zz + nz - z) % nz
        is_up = (offset == 0) | (offset >= half)

        @pl.when(is_up)
        def _():
            xcopy(1, x_r, zz, x_l).wait_recv()
            for lane in range(2):
                ycopy(lane, 1, y_r, zz, y_l).wait_recv()

        @pl.when(jnp.logical_not(is_up))
        def _():
            xcopy(0, x_l, zz, x_r).wait_recv()
            for lane in range(2):
                ycopy(lane, 0, y_l, zz, y_r).wait_recv()

        xcopy(2, x_o, zz, x_r).wait_recv()
        for lane in range(2):
            ycopy(lane, 2, y_o, zz, y_r).wait_recv()
        return carry

    lax.fori_loop(0, nz, collect, 0)

    send_o = pltpu.make_async_remote_copy(
        bigo.at[c], bigo.at[c], p_send.at[1], p_recv.at[1], device_id=partner, device_id_type=MESH
    )
    send_o.start()
    send_normed.wait_recv()

    def weight(t):
        return jnp.concatenate([big[t + j].reshape(D, 128) for j in range(3)], axis=1)

    def project(t, row):
        return mm(normed[pl.ds(row, BLOCK), :], weight(t))

    for b in range(2):
        keys[BLOCK * (b + 1) : BLOCK * (b + 2), :] = project(3, BLOCK * b).astype(BF16)
        values[BLOCK * (b + 1) : BLOCK * (b + 2), :] = project(6, BLOCK * b).astype(BF16)

    first, last = place == 0, place == 7
    halos = []
    for k, ref in enumerate((keys, values)):
        halos.append(
            pltpu.make_async_remote_copy(
                ref.at[pl.ds(BLOCK, BLOCK), :],
                ref.at[pl.ds(3 * BLOCK, BLOCK), :],
                h_send.at[k, 0],
                h_recv.at[k, 0],
                device_id=dev_prev,
                device_id_type=MESH,
            )
        )
        halos.append(
            pltpu.make_async_remote_copy(
                ref.at[pl.ds(2 * BLOCK, BLOCK), :],
                ref.at[pl.ds(0, BLOCK), :],
                h_send.at[k, 1],
                h_recv.at[k, 1],
                device_id=dev_next,
                device_id_type=MESH,
            )
        )

    @pl.when(jnp.logical_not(first))
    def _():
        halos[0].start()
        halos[2].start()

    @pl.when(jnp.logical_not(last))
    def _():
        halos[1].start()
        halos[3].start()

    @pl.when(first)
    def _():
        keys[0:BLOCK, :] = jnp.zeros((BLOCK, HALF), BF16)
        values[0:BLOCK, :] = jnp.zeros((BLOCK, HALF), BF16)

    @pl.when(last)
    def _():
        keys[3 * BLOCK : 4 * BLOCK, :] = jnp.zeros((BLOCK, HALF), BF16)
        values[3 * BLOCK : 4 * BLOCK, :] = jnp.zeros((BLOCK, HALF), BF16)

    bias_c = bias_ref[pl.ds(c, 1), :]
    bias_p = bias_ref[pl.ds(2 + c, 1), :]
    for b in range(2):
        query = project(0, BLOCK * b).astype(BF16).astype(F32)
        with_c[BLOCK * b : BLOCK * (b + 1), :] = (query + bias_c).astype(BF16)
        with_p[BLOCK * b : BLOCK * (b + 1), :] = (query + bias_p).astype(BF16)

    def rcopy(kind, row, count, to):
        view = rel.at[pl.ds(pl.multiple_of(row, 16), count), :]
        return pltpu.make_async_remote_copy(
            view,
            view,
            rx_send.at[kind],
            rx_recv.at[kind],
            device_id=dev(to, y, z, c),
            device_id_type=MESH,
        )

    @pl.when(c == y_lo)
    def _():
        rel_here.wait()

    def rel_wait(core):
        pltpu.make_async_remote_copy(
            rel_own,
            rel.at[pl.ds(pl.multiple_of(x * HS + core * 48, 16), 48), :],
            ra_send.at[0],
            ra_recv.at[core],
            device_id=partner,
            device_id_type=MESH,
        ).wait_recv()

    rel_wait(1 - c)

    @pl.when(c != y_lo)
    def _():
        rel_wait(c)

    rcopy(0, x * HS, HS, x_r).start()
    rcopy(1, x * HS, HS, x_l).start()
    rcopy(0, x_l * HS, HS, x_r).wait_recv()
    rcopy(2, x_l * HS, 48, x_r).start()
    rcopy(1, x_r * HS, HS, x_l).wait_recv()
    rcopy(3, x_r * HS + 48, 48, x_l).start()
    rcopy(2, x_o * HS, 48, x_r).wait_recv()
    rcopy(3, x_o * HS + 48, 48, x_l).wait_recv()

    @pl.when(jnp.logical_not(last))
    def _():
        halos[0].wait_recv()
        halos[2].wait_recv()

    @pl.when(jnp.logical_not(first))
    def _():
        halos[1].wait_recv()
        halos[3].wait_recv()

    valid_len = len_ref[0]
    scale = 1.0 / math.sqrt(HS)
    windows = ((0, 128), (0, 256), (128, 384), (256, 384))
    send_ctx = pltpu.make_async_remote_copy(
        ctx_out, ctx.at[c], p_send.at[2], p_recv.at[2], device_id=partner, device_id_type=MESH
    )

    def attend(i, carry):
        b = jnp.where(i == 0, 1 - c, c)
        row = pl.multiple_of(b * BLOCK, BLOCK)
        first_pos = place * (2 * BLOCK) + row
        key_pos = first_pos - BLOCK + lax.broadcasted_iota(jnp.int32, (1, 3 * BLOCK), 1)
        key_valid = (key_pos >= 0) & (key_pos < valid_len)
        query_pos = first_pos + lax.broadcasted_iota(jnp.int32, (BLOCK, 1), 0)
        parts = []
        for h, (lo, hi) in enumerate(windows):
            lane = lo + lax.broadcasted_iota(jnp.int32, (BLOCK, hi - lo), 1)
            mine = (lane >= HS * h) & (lane < HS * (h + 1))
            zero = jnp.zeros((BLOCK, hi - lo), BF16)
            qc = jnp.where(mine, with_c[pl.ds(row, BLOCK), lo:hi], zero)
            qp = jnp.where(mine, with_p[pl.ds(row, BLOCK), lo:hi], zero)
            position = mm(qp, rel[lo:hi, :])
            shifted = pltpu.roll(position, 3 * BLOCK + 1, 1, stride=1, stride_axis=0)[:, : 3 * BLOCK]
            score = mm_t(qc, keys[pl.ds(row, 3 * BLOCK), lo:hi]) + shifted
            score = jnp.where(key_valid, score, masked_score)
            raised = jnp.exp((score - jnp.max(score, axis=1, keepdims=True)) * scale)
            total = jnp.sum(raised, axis=1, keepdims=True)
            inverse = jnp.where(query_pos < valid_len, 1.0 / total, 0.0)
            parts.append(mm(raised.astype(BF16), values[pl.ds(row, 3 * BLOCK), lo:hi]) * inverse)
        lane = lax.broadcasted_iota(jnp.int32, (BLOCK, 128), 1)
        tiles = (
            jnp.where(lane < 96, parts[0], parts[1][:, :128]),
            jnp.where(lane < 64, parts[1][:, 128:], parts[2][:, :128]),
            jnp.where(lane < 32, parts[2][:, 128:], parts[3]),
        )

        @pl.when(i == 0)
        def _():
            for j, tile in enumerate(tiles):
                ctx_out[:, 128 * j : 128 * (j + 1)] = tile.astype(BF16)
            send_ctx.start()

        @pl.when(i == 1)
        def _():
            for j, tile in enumerate(tiles):
                ctx[c, :, 128 * j : 128 * (j + 1)] = tile.astype(BF16)

        return carry

    lax.fori_loop(0, 2, attend, 0)

    pltpu.make_async_remote_copy(
        bigo.at[1 - c],
        bigo.at[1 - c],
        p_send.at[1],
        p_recv.at[1],
        device_id=partner,
        device_id_type=MESH,
    ).wait_recv()
    pltpu.make_async_remote_copy(
        ctx_out, ctx.at[1 - c], p_send.at[2], p_recv.at[2], device_id=partner, device_id_type=MESH
    ).wait_recv()

    for g in range(2):
        for j in range(0, 6, 2):
            total = None
            for k in range(2):
                w = jnp.concatenate([bigo[g, j, k], bigo[g, j + 1, k]], axis=1)
                part = mm(ctx[k], w)
                total = part if total is None else total + part
            at = g * 768 + j * 128
            out_ref[:, at : at + 256] = (frames_ref[:, at : at + 256].astype(F32) + total).astype(BF16)

    for cp in stage0:
        cp.wait_send()
    send_normed.wait_send()
    send_o.wait_send()
    send_ctx.wait_send()
    rel_cross.wait_send()

    @pl.when(c != y_lo)
    def _():
        rel_across.wait_send()

    rcopy(0, x * HS, HS, x_r).wait_send()
    rcopy(1, x * HS, HS, x_l).wait_send()
    rcopy(2, x_l * HS, 48, x_r).wait_send()
    rcopy(3, x_r * HS + 48, 48, x_l).wait_send()

    @pl.when(jnp.logical_not(first))
    def _():
        halos[0].wait_send()
        halos[2].wait_send()

    @pl.when(jnp.logical_not(last))
    def _():
        halos[1].wait_send()
        halos[3].wait_send()

    def drain(zz, carry):
        offset = (zz + nz - z) % nz
        is_up = (offset == 0) | (offset > half)
        for lane in range(5):

            @pl.when(is_up)
            def _():
                zcopy(lane, 0, zz).wait_send()

            @pl.when(offset < half - 1)
            def _():
                zcopy(lane, 1, zz).wait_send()

        for kind in range(3):
            xcopy(kind, x, zz, x_r).wait_send()
            for lane in range(2):
                ycopy(lane, kind, y, zz, y_r).wait_send()
        return carry

    lax.fori_loop(0, nz, drain, 0)


def attention_block(nz, frames, lengths, gain, wq, wk, wv, wo, wpos, bias, table):
    vmem = pl.BlockSpec(memory_space=pltpu.VMEM)
    hbm = pl.BlockSpec(memory_space=pl.ANY)
    smem = pl.BlockSpec(memory_space=pltpu.SMEM)
    dma = pltpu.SemaphoreType.DMA
    rows = nz * 48
    return pl.pallas_call(
        lambda *refs: kernel(nz, *refs),
        out_shape=jax.ShapeDtypeStruct((BLOCK, D), BF16),
        in_specs=[vmem, smem, vmem, hbm, hbm, hbm, hbm, vmem, vmem, vmem],
        out_specs=vmem,
        scratch_shapes=[
            pltpu.VMEM((2 * BLOCK, D), BF16),
            pltpu.VMEM((9, 48, 128), BF16),
            pltpu.VMEM((6, 24, 128), BF16),
            pltpu.VMEM((9, 2, rows, 128), BF16),
            pltpu.VMEM((2, 6, 2, nz * 24, 128), BF16),
            pltpu.VMEM((STEP_ROWS, D), BF16),
            pltpu.VMEM((48, 1024), BF16),
            pltpu.VMEM((HALF, 1024), BF16),
            pltpu.VMEM((4 * BLOCK, HALF), BF16),
            pltpu.VMEM((4 * BLOCK, HALF), BF16),
            pltpu.VMEM((2 * BLOCK, HALF), BF16),
            pltpu.VMEM((2 * BLOCK, HALF), BF16),
            pltpu.VMEM((BLOCK, HALF), BF16),
            pltpu.VMEM((2, BLOCK, HALF), BF16),
            dma((15,)),
            dma((6,)),
            dma((6,)),
            dma((2, 5, nz)),
            dma((5, nz)),
            dma((3, nz)),
            dma((3, nz)),
            dma((2, 3, nz)),
            dma((2, 3, nz)),
            dma((2,)),
            dma((2,)),
            dma((4,)),
            dma((4,)),
            dma((2, 2)),
            dma((2, 2)),
            dma((3,)),
            dma((3,)),
        ],
        compiler_params=pltpu.CompilerParams(
            collective_id=0, has_side_effects=True, vmem_limit_bytes=60 * 1024 * 1024
        ),
        name="attention_block",
    )(frames, lengths, gain, wq, wk, wv, wo, wpos, bias, table)


def angle_tables():
    frequency = jnp.exp(jnp.arange(D // 2, dtype=F32) * (-2.0 * math.log(10000.0) / D))
    steps = jnp.arange(GROUP, dtype=F32)
    coarse = (steps * GROUP - (2 * BLOCK - 1))[:, None] * frequency[None, :]
    fine = steps[:, None] * frequency[None, :]
    return jnp.stack([jnp.sin(coarse), jnp.cos(coarse), jnp.sin(fine), jnp.cos(fine)])


def solution(mesh):
    nz = mesh.shape["dp"] // 2

    def body(
        frames, lengths, ln_gain, w_query, w_key, w_value, w_output, w_position, bias_c, bias_p
    ):
        bias = jnp.concatenate([bias_c.reshape(2, HALF), bias_p.reshape(2, HALF)])
        out = attention_block(
            nz,
            frames[0],
            lengths,
            ln_gain.reshape(1, D),
            w_query,
            w_key,
            w_value,
            w_output,
            w_position,
            bias,
            angle_tables(),
        )
        return out[None]

    placed = (
        P("dp", "tm", None),
        P("dp"),
        P(),
        P("dp", None),
        P("dp", None),
        P("dp", None),
        P("dp", None),
        P(None, "tm"),
        P(),
        P(),
    )
    return jax.shard_map(
        body, mesh=mesh, in_specs=placed, out_specs=P("dp", "tm", None), check_vma=False
    )
```
